256 devices in a mesh: grp: 8 (over x, core), mem: 32 (over y, z).
Axes of the slice: x: 4, y: 4, z: 8, core: 2. Of those that a mesh axis runs over, the one named last changes fastest.
Arguments:
- child_field: float32 [2, 1024, 32768], P(None, None, ('grp', 'mem')), may hold values from -6 to 6
- theta_interp: float32 [64, 32], replicated, may hold values from -1 to 1
- phi_interp: float32 [64, 32], replicated, may hold values from -1 to 1
- child_phase: float32 [8, 4096], replicated, may hold values from -3.140625 to 3.140625
- translation: float32 [2, 316, 4096], P(None, None, 'mem'), may hold values from -0.3125 to 0.3125
- inter_source: int32 [256, 24], P('grp'), may hold values from 0 to 255, as said below
- inter_kind: int32 [256, 24], P('grp'), may hold values from 0 to 315
- inter_count: int32 [256], P('grp'), may hold values from 6 to 24
Outputs:
- child_out: float32 [2, 1024, 32768], P(None, None, ('grp', 'mem'))
The draws below stay inside these ranges and needn't reach their ends.
Inputs may be any that keep to these rules, and one draw needn't show every extreme that they name: The source box of every slot lies in its target's group of 32 consecutive parent boxes or in one of the two groups beside it: inter_source[t, k] // 32 differs from t // 32 by at most one. Slots from inter_count[t] on are unused.
All inputs are finite; a program needn't handle non-finite values.
Results may differ from the reference program's by a relative error of at most 0.0003.
Values sent between devices are 32-bit elements; how exact they have to be, the bound alone decides.
A program may use at most 64 MiB of HBM per device.

```python
import jax
import jax.numpy as jnp
from jax import lax

L1T = 32
L1P = 32
L2T = 64
L2P = 64
SAMPLES1 = 1024
SAMPLES2 = 4096
WAVES = 16
BRANCH = 8
SLOTS = 24
NTRANS = 316
GROUPS = 8
GROUP_PARENTS = 32
PARENTS = 256
CHILDREN = 2048


def draw_inter_source(key, part):
    first_key, second_key = jax.random.split(jax.random.fold_in(key, 11))
    target_group = (jnp.arange(PARENTS, dtype=jnp.int32) // GROUP_PARENTS)[:, None]
    stepping = jax.random.randint(first_key, (PARENTS, SLOTS), -1, 2)
    source_group = jnp.clip(target_group + stepping, 0, GROUPS - 1)
    member_pick = jax.random.randint(second_key, (PARENTS, SLOTS), 0, GROUP_PARENTS)
    return (source_group * GROUP_PARENTS + member_pick).astype(jnp.int32)


def plant(entries, own_key, smallest, largest):
    longest = entries.shape.index(max(entries.shape))
    spots = []
    for shift in (0, 1):
        where = [jax.random.randint(jax.random.fold_in(own_key, axis), (), 0, length) for axis, length in enumerate(entries.shape)]
        where[longest] = (where[longest] + shift) % entries.shape[longest]
        spots.append(tuple(where))
    return entries.at[spots[0]].set(smallest).at[spots[1]].set(largest)


def level_of(own_key, extent, cuts, low, largest):
    gain = 1.0
    for axis_at, blocks in cuts:
        steps = jax.random.uniform(jax.random.fold_in(jax.random.fold_in(own_key, 6), axis_at), (blocks,), jnp.float32, low / len(cuts), largest / len(cuts))
        gain = gain * jnp.repeat(jnp.exp(steps), extent[axis_at] // blocks).reshape((-1,) + (1,) * (len(extent) - 1 - axis_at))
    return gain


def normal_values(stream_key, dims, width, bound, cuts=(), held_as=jnp.bfloat16):
    array = width * jax.random.normal(stream_key, dims, jnp.float32)
    if cuts:
        array = array * level_of(stream_key, dims, cuts, -0.22, 0.18)
    return jnp.clip(array, -bound, bound).astype(held_as)


def setup_inputs(seed: int = 0) -> dict:
    key_of = jax.random.split(jax.random.key(seed), 9)
    return {
        "child_field": normal_values(key_of[0], (2, SAMPLES1, CHILDREN * WAVES), 1.0, 6.0, ((2, 256),), jnp.float32),
        "theta_interp": normal_values(key_of[1], (L2T, L1T), L1T ** -0.5, 1.0, (), jnp.float32),
        "phi_interp": normal_values(key_of[2], (L2P, L1P), L1P ** -0.5, 1.0, (), jnp.float32),
        "child_phase": jnp.clip(jax.random.uniform(key_of[3], (BRANCH, SAMPLES2), jnp.float32, -3.140625, 3.140625), -3.140625, 3.140625),
        "translation": normal_values(key_of[4], (2, NTRANS, SAMPLES2), (16 * SLOTS) ** -0.5, 0.3125, ((2, 32),), jnp.float32),
        "inter_source": draw_inter_source(jax.random.fold_in(key_of[8], 71), 0),
        "inter_kind": plant(jax.random.randint(key_of[6], (PARENTS, SLOTS), 0, NTRANS), jax.random.fold_in(key_of[6], 1), 0, NTRANS - 1).astype(jnp.int32),
        "inter_count": plant(jax.random.randint(key_of[7], (PARENTS,), SLOTS // 4, SLOTS + 1), jax.random.fold_in(key_of[7], 1), SLOTS // 4, SLOTS).astype(jnp.int32),
    }


precise = lax.Precision.HIGHEST


def spread_out(samples, theta_interp, phi_interp):
    columns = samples.shape[2]
    arranged = samples.reshape(2, theta_interp.shape[1], phi_interp.shape[1], columns)
    middle = jnp.einsum("at,ctpr->capr", theta_interp, arranged, precision=precise)
    fine_grid = jnp.einsum("bp,capr->cabr", phi_interp, middle, precision=precise)
    return fine_grid.reshape(2, theta_interp.shape[0] * phi_interp.shape[0], columns)


def fold_back(samples, theta_interp, phi_interp):
    columns = samples.shape[2]
    arranged = samples.reshape(2, theta_interp.shape[0], phi_interp.shape[0], columns)
    middle = jnp.einsum("bp,cabr->capr", phi_interp, arranged, precision=precise)
    coarse = jnp.einsum("at,capr->ctpr", theta_interp, middle, precision=precise)
    return coarse.reshape(2, theta_interp.shape[1] * phi_interp.shape[1], columns)


def reference(child_field, theta_interp, phi_interp, child_phase, translation, inter_source, inter_kind, inter_count):
    branch = child_phase.shape[0]
    cosine = jnp.cos(child_phase).T[:, :, None]
    sine_table = jnp.sin(child_phase).T[:, :, None]
    block_width = branch * WAVES
    parent_ids = jnp.arange(PARENTS, dtype=jnp.int32)

    def gather_parent(parent):
        child_block = lax.dynamic_slice_in_dim(child_field, parent * block_width, block_width, 2)
        fine_grid = spread_out(child_block, theta_interp, phi_interp)
        grouped = fine_grid.reshape(2, fine_grid.shape[1], branch, WAVES)
        real_part = grouped[0] * cosine - grouped[1] * sine_table
        imag_part = grouped[1] * cosine + grouped[0] * sine_table
        return jnp.stack([jnp.sum(real_part, axis=1), jnp.sum(imag_part, axis=1)])

    outgoing = lax.map(gather_parent, parent_ids)
    slot_index = jnp.arange(SLOTS, dtype=jnp.int32)

    def translate_one(pieces):
        sources, kind_rows, live_count = pieces
        weight = (slot_index < live_count).astype(jnp.float32)
        picked = jnp.take(outgoing, sources, axis=0)
        factor = jnp.take(translation, kind_rows, axis=1) * weight[None, :, None]
        real_part = jnp.sum(factor[0][:, :, None] * picked[:, 0] - factor[1][:, :, None] * picked[:, 1], axis=0)
        imag_part = jnp.sum(factor[0][:, :, None] * picked[:, 1] + factor[1][:, :, None] * picked[:, 0], axis=0)
        return jnp.stack([real_part, imag_part])

    incoming = lax.map(translate_one, (inter_source, inter_kind, inter_count))

    def scatter_parent(parent):
        parent_field = incoming[parent]
        real_part = parent_field[0][:, None, :] * cosine + parent_field[1][:, None, :] * sine_table
        imag_part = parent_field[1][:, None, :] * cosine - parent_field[0][:, None, :] * sine_table
        local_field = jnp.stack([real_part, imag_part]).reshape(2, parent_field.shape[1], block_width)
        return fold_back(local_field, theta_interp, phi_interp)

    blocks = lax.map(scatter_parent, parent_ids)
    return jnp.transpose(blocks, (1, 2, 0, 3)).reshape(2, SAMPLES1, PARENTS * block_width)
```

```python
import functools
import math

import jax
import jax.numpy as jnp
from jax import lax
from jax.experimental import pallas as pl
from jax.experimental.pallas import tpu as pltpu
from jax.sharding import PartitionSpec as P

MESH = pl.DeviceIdType.MESH
f32 = jnp.float32
bf16 = jnp.bfloat16


def two_terms(x):
    high = x.astype(bf16)
    return high, (x - high.astype(f32)).astype(bf16)


def dot(a, b):
    return jnp.dot(a, b, preferred_element_type=f32)


def dot_rows(a, b):
    return lax.dot_general(a, b, (((1,), (1,)), ((), ())), preferred_element_type=f32)


def where_true(rows, cols, test):
    r = lax.broadcasted_iota(jnp.int32, (rows, cols), 0)
    c = lax.broadcasted_iota(jnp.int32, (rows, cols), 1)
    return jnp.where(test(r, c), 1.0, 0.0).astype(f32)


def sine_and_cosine(q):
    y = 0.5 * q
    z = y * y
    s = 0.0
    for n in (11, 9, 7, 5, 3, 1):
        s = s * z + (-1.0) ** (n // 2) / math.factorial(n)
    c = 0.0
    for n in (12, 10, 8, 6, 4, 2, 0):
        c = c * z + (-1.0) ** (n // 2) / math.factorial(n)
    s = s * y
    return 2.0 * s * c, 1.0 - 2.0 * s * s


def body(
    dims,
    x_ref,
    theta_ref,
    phi_ref,
    phase_ref,
    trans_ref,
    source_ref,
    kind_ref,
    count_ref,
    out_ref,
    cos_ref,
    sin_ref,
    mid_ref,
    back_ref,
    spread_lhs,
    spread_rhs,
    fold_lhs,
    fold_rhs,
    table_ref,
    give_ref,
    hold_ref,
    result_ref,
    take_ref,
    give_sem,
    hold_sem,
    pass_sem,
    side_sem,
    result_sem,
    take_sem,
):
    groups, members, coarse_t, coarse_p, fine_t, fine_p, branch, waves, slots, kinds = dims
    pairs = members // 2
    lanes = 2 * fine_p
    columns = branch * waves
    me = lax.axis_index("mem")
    group = lax.axis_index("grp")
    right = lax.rem(group + 1, groups)
    left = lax.rem(group + groups - 1, groups)

    barrier = pltpu.get_barrier_semaphore()

    def greet(k, carry):
        pl.semaphore_signal(
            barrier, inc=1, device_id={"mem": lax.rem(me + k, members)}, device_id_type=MESH
        )
        return carry

    lax.fori_loop(1, members, greet, 0)
    for other in (left, right):
        pl.semaphore_signal(barrier, inc=1, device_id={"grp": other}, device_id_type=MESH)

    def pair_at(k, sign):
        if pairs == 16:
            step = lax.rem(11 * (k + 1), 16)
            home = me // 2
            y = lax.rem(home // 4 + 4 + sign * (step // 4), 4)
            z = lax.rem(lax.rem(home, 4) + 4 + sign * lax.rem(step, 4), 4)
            return 4 * y + z
        return lax.rem(me // 2 + pairs + sign * lax.rem(k + 1, pairs), pairs)

    theta_high, theta_low = two_terms(theta_ref[...])
    phi_high, phi_low = two_terms(phi_ref[...])
    at = lambda rows, cols, test: where_true(rows, cols, test).astype(bf16)
    spread_lhs[...] = (
        dot(theta_high, at(coarse_t, 3 * coarse_t, lambda r, c: (c == r) | (c == r + coarse_t)))
        + dot(theta_low, at(coarse_t, 3 * coarse_t, lambda r, c: c == r + 2 * coarse_t))
    ).astype(bf16)
    own = where_true(4 * coarse_p, 4 * fine_p, lambda r, c: r // coarse_p == c // fine_p)
    rows_p = at(4 * coarse_p, coarse_p, lambda r, c: (r & (coarse_p - 1)) == c)
    cols_b = at(fine_p, 4 * fine_p, lambda r, c: r == (c & (fine_p - 1)))
    for n, term in enumerate((phi_high, phi_low)):
        small = dot_rows(rows_p, term).astype(bf16)
        spread_rhs[n] = (dot(small, cols_b) * own).astype(bf16)

    def angles(i, carry):
        at_lanes = pl.ds(pl.multiple_of(i * 2 * lanes, 2 * lanes), 2 * lanes)
        s, c = sine_and_cosine(phase_ref[:, at_lanes])
        sin_ref[:, at_lanes] = s
        cos_ref[:, at_lanes] = c
        return carry

    lax.fori_loop(0, pairs, angles, 0)

    lhs = spread_lhs[...]

    def theta_step(p, carry):
        terms = [two_terms(x_ref[n, pl.ds(p, coarse_t, stride=coarse_p), :]) for n in range(2)]
        high = jnp.concatenate([terms[0][0], terms[1][0]], axis=1)
        low = jnp.concatenate([terms[0][1], terms[1][1]], axis=1)
        made = dot(lhs, jnp.concatenate([high, low, high], axis=0))
        for n in range(2):
            mid_ref[n, pl.ds(p, fine_t, stride=coarse_p), :] = made[
                :, n * columns : (n + 1) * columns
            ]
        return carry

    lax.fori_loop(0, coarse_p, theta_step, 0, unroll=8)

    pl.semaphore_wait(barrier, members + 1)

    def give_copy(to):
        return pltpu.make_async_remote_copy(
            src_ref=give_ref.at[to],
            dst_ref=hold_ref.at[members + me],
            send_sem=give_sem.at[to],
            recv_sem=hold_sem.at[me],
            device_id={"mem": to},
            device_id_type=MESH,
        )

    def spread_pair(k, carry):
        pair = pair_at(k, 1)
        rows = pl.ds(pl.multiple_of(pair * 4 * coarse_p, 4 * coarse_p), 4 * coarse_p)
        turned = jnp.concatenate([mid_ref[0, rows, :].T, mid_ref[1, rows, :].T], axis=0)
        high, low = two_terms(turned)
        both = jnp.concatenate([spread_rhs[0], spread_rhs[0]], axis=0)
        fine = dot(jnp.concatenate([high, low], axis=1), both) + dot(high, spread_rhs[1])
        at_lanes = pl.ds(pl.multiple_of(pair * 2 * lanes, 2 * lanes), 2 * lanes)
        cosine = cos_ref[:, at_lanes]
        sine = sin_ref[:, at_lanes]
        real = imag = 0.0
        for j in range(branch):
            re = fine[j * waves : (j + 1) * waves]
            im = fine[columns + j * waves : columns + (j + 1) * waves]
            c, s = cosine[j : j + 1], sine[j : j + 1]
            real = real + (re * c - im * s)
            imag = imag + (im * c + re * s)
        for side in range(2):
            to = 2 * pair + side
            cut = slice(side * lanes, (side + 1) * lanes)
            block = (real[:, cut].reshape(2, waves // 2, lanes), imag[:, cut].reshape(2, waves // 2, lanes))
            for n in range(2):
                give_ref[to, n] = block[n]

            @pl.when(to != me)
            def _():
                give_copy(to).start()

            @pl.when(to == me)
            def _():
                for n in range(2):
                    hold_ref[members + me, n] = block[n]

        return carry

    lax.fori_loop(0, pairs, spread_pair, 0)

    def table_step(i, carry):
        for n in range(2):
            table_ref[i, n] = jnp.broadcast_to(trans_ref[n, pl.ds(i, 1), :], (waves // 2, lanes))
        return carry

    lax.fori_loop(0, kinds, table_step, 0)
    table_ref[kinds] = jnp.zeros((2, waves // 2, lanes), f32)

    def pass_copy(box, way):
        to = right if way == 0 else left
        return pltpu.make_async_remote_copy(
            src_ref=hold_ref.at[members + box],
            dst_ref=hold_ref.at[2 * members * way + box],
            send_sem=pass_sem.at[way, box],
            recv_sem=side_sem.at[way],
            device_id={"grp": to},
            device_id_type=MESH,
        )

    def pass_pair(k, carry):
        pair = pair_at(k, -1)
        for side in range(2):
            box = 2 * pair + side

            @pl.when(box != me)
            def _():
                pltpu.make_async_remote_copy(
                    src_ref=give_ref.at[box],
                    dst_ref=hold_ref.at[members + box],
                    send_sem=give_sem.at[box],
                    recv_sem=hold_sem.at[box],
                    device_id={"mem": box},
                    device_id_type=MESH,
                ).wait_recv()

            for way in range(2):
                pass_copy(box, way).start()
        return carry

    lax.fori_loop(0, pairs, pass_pair, 0)

    own_back = where_true(4 * fine_p, 4 * coarse_p, lambda r, c: r // fine_p == c // coarse_p)
    rows_b = at(4 * fine_p, fine_p, lambda r, c: (r & (fine_p - 1)) == c)
    cols_p = at(coarse_p, 4 * coarse_p, lambda r, c: r == (c & (coarse_p - 1)))
    for n, term in enumerate((phi_high, phi_low)):
        small = dot(rows_b, term).astype(bf16)
        fold_rhs[:, n * 4 * coarse_p : (n + 1) * 4 * coarse_p] = (
            dot(small, cols_p) * own_back
        ).astype(bf16)
    eye = at(coarse_t, coarse_t, lambda r, c: r == c)
    turned_high = dot_rows(eye, theta_high).astype(bf16)
    turned_low = dot_rows(eye, theta_low).astype(bf16)
    fold_lhs[...] = (
        dot(turned_high, at(fine_t, 3 * fine_t, lambda r, c: (c == r) | (c == r + fine_t)))
        + dot(turned_low, at(fine_t, 3 * fine_t, lambda r, c: c == r + 2 * fine_t))
    ).astype(bf16)

    for way in range(2):
        span = pl.ds(2 * members * way, members)
        pltpu.make_async_remote_copy(
            src_ref=hold_ref.at[span],
            dst_ref=hold_ref.at[span],
            send_sem=pass_sem.at[way, 0],
            recv_sem=side_sem.at[way],
            device_id={"grp": right},
            device_id_type=MESH,
        ).wait_recv()

    base = (group - 1) * members

    def translate(k, carry):
        target = 2 * pair_at(k // 2, 1) + lax.rem(k, 2)
        live = count_ref[target]
        real = jnp.zeros((2, waves // 2, lanes), f32)
        imag = jnp.zeros((2, waves // 2, lanes), f32)
        for slot in range(slots):
            used = slot < live
            source = jnp.where(used, source_ref[target, slot] - base, members)
            kind = jnp.where(used, kind_ref[target, slot], kinds)
            box = hold_ref[source]
            factor = table_ref[kind]
            real = real + (factor[0] * box[0] - factor[1] * box[1])
            imag = imag + (factor[0] * box[1] + factor[1] * box[0])
        result_ref[target, 0] = real
        result_ref[target, 1] = imag

        @pl.when(target != me)
        def _():
            pltpu.make_async_remote_copy(
                src_ref=result_ref.at[target],
                dst_ref=take_ref.at[me],
                send_sem=result_sem.at[target],
                recv_sem=take_sem.at[me],
                device_id={"mem": target},
                device_id_type=MESH,
            ).start()

        @pl.when(target == me)
        def _():
            take_ref[me, 0] = real
            take_ref[me, 1] = imag

        return carry

    lax.fori_loop(0, members, translate, 0)

    def fold_pair(k, carry):
        pair = pair_at(k, -1)
        for side in range(2):
            box = 2 * pair + side

            @pl.when(box != me)
            def _():
                pltpu.make_async_remote_copy(
                    src_ref=result_ref.at[box],
                    dst_ref=take_ref.at[box],
                    send_sem=result_sem.at[box],
                    recv_sem=take_sem.at[box],
                    device_id={"mem": box},
                    device_id_type=MESH,
                ).wait_recv()

        at_lanes = pl.ds(pl.multiple_of(pair * 2 * lanes, 2 * lanes), 2 * lanes)
        cosine = cos_ref[:, at_lanes]
        sine = sin_ref[:, at_lanes]
        re, im = (
            jnp.concatenate(
                [take_ref[2 * pair + side, n].reshape(waves, lanes) for side in range(2)], axis=1
            )
            for n in range(2)
        )
        parts = [[], []]
        for j in range(branch):
            c, s = cosine[j : j + 1], sine[j : j + 1]
            parts[0].append(re * c + im * s)
            parts[1].append(im * c - re * s)
        high, low = two_terms(jnp.concatenate(parts[0] + parts[1], axis=0))
        wide = dot(high, fold_rhs[...])
        width = 4 * coarse_p
        made = wide[:, :width] + wide[:, width:] + dot(low, fold_rhs[:, :width])
        rows = pl.ds(pl.multiple_of(pair * width, width), width)
        for n in range(2):
            back_ref[n, rows, :] = made[n * columns : (n + 1) * columns].T
        return carry

    lax.fori_loop(0, pairs, fold_pair, 0)

    lhs_back = fold_lhs[...]

    def fold_step(p, carry):
        terms = [two_terms(back_ref[n, pl.ds(p, fine_t, stride=coarse_p), :]) for n in range(2)]
        high = jnp.concatenate([terms[0][0], terms[1][0]], axis=1)
        low = jnp.concatenate([terms[0][1], terms[1][1]], axis=1)
        made = dot(lhs_back, jnp.concatenate([high, low, high], axis=0))
        for n in range(2):
            out_ref[n, pl.ds(p, coarse_t, stride=coarse_p), :] = made[
                :, n * columns : (n + 1) * columns
            ]
        return carry

    lax.fori_loop(0, coarse_p, fold_step, 0, unroll=8)

    def sent(k, carry):
        to = lax.rem(me + k, members)
        give_copy(to).wait_send()
        pltpu.make_async_remote_copy(
            src_ref=result_ref.at[to],
            dst_ref=take_ref.at[me],
            send_sem=result_sem.at[to],
            recv_sem=take_sem.at[me],
            device_id={"mem": to},
            device_id_type=MESH,
        ).wait_send()
        return carry

    lax.fori_loop(1, members, sent, 0)

    def passed(box, carry):
        for way in range(2):
            pass_copy(box, way).wait_send()
        return carry

    lax.fori_loop(0, members, passed, 0)


def per_device(groups, members, waves, *arrays):
    field, theta, phi, phase, trans, source, kind, count = arrays
    fine_t, coarse_t = theta.shape
    fine_p, coarse_p = phi.shape
    branch = phase.shape[0]
    slots = source.shape[1]
    kinds = trans.shape[1]
    columns = field.shape[2]
    lanes = trans.shape[2]
    dims = (groups, members, coarse_t, coarse_p, fine_t, fine_p, branch, waves, slots, kinds)
    block = (2, 2, waves // 2, lanes)
    in_vmem = pl.BlockSpec(memory_space=pltpu.VMEM)
    in_smem = pl.BlockSpec(memory_space=pltpu.SMEM)
    return pl.pallas_call(
        functools.partial(body, dims),
        out_shape=jax.ShapeDtypeStruct(field.shape, f32),
        in_specs=[in_vmem] * 5 + [in_smem] * 3,
        out_specs=in_vmem,
        scratch_shapes=[
            pltpu.VMEM(phase.shape, f32),
            pltpu.VMEM(phase.shape, f32),
            pltpu.VMEM((2, fine_t * coarse_p, columns), f32),
            pltpu.VMEM((2, fine_t * coarse_p, columns), f32),
            pltpu.VMEM((fine_t, 3 * coarse_t), bf16),
            pltpu.VMEM((2, 4 * coarse_p, 4 * fine_p), bf16),
            pltpu.VMEM((coarse_t, 3 * fine_t), bf16),
            pltpu.VMEM((4 * fine_p, 8 * coarse_p), bf16),
            pltpu.VMEM((kinds + 1, 2, waves // 2, lanes), f32),
            pltpu.VMEM((members, *block), f32),
            pltpu.VMEM((3 * members, *block), f32),
            pltpu.VMEM((members, *block), f32),
            pltpu.VMEM((members, *block), f32),
            pltpu.SemaphoreType.DMA((members,)),
            pltpu.SemaphoreType.DMA((members,)),
            pltpu.SemaphoreType.DMA((2, members)),
            pltpu.SemaphoreType.DMA((2,)),
            pltpu.SemaphoreType.DMA((members,)),
            pltpu.SemaphoreType.DMA((members,)),
        ],
        compiler_params=pltpu.CompilerParams(
            collective_id=0, has_side_effects=True, vmem_limit_bytes=40 << 20
        ),
    )(field, theta, phi, phase, trans, source, kind, count)


def solution(mesh):
    groups, members = mesh.shape["grp"], mesh.shape["mem"]

    def run(field, theta, phi, phase, trans, source, kind, count):
        waves = field.shape[2] // phase.shape[0]
        return per_device(
            groups, members, waves, field, theta, phi, phase, trans, source, kind, count
        )

    return jax.shard_map(
        run,
        mesh=mesh,
        in_specs=(
            P(None, None, ("grp", "mem")),
            P(),
            P(),
            P(),
            P(None, None, "mem"),
            P("grp", None),
            P("grp", None),
            P("grp"),
        ),
        out_specs=P(None, None, ("grp", "mem")),
        check_vma=False,
    )
```

```python
import functools
import math

import jax
import jax.numpy as jnp
from jax import lax
from jax.experimental import pallas as pl
from jax.experimental.pallas import tpu as pltpu
from jax.sharding import PartitionSpec as P

MESH = pl.DeviceIdType.MESH
f32 = jnp.float32
bf16 = jnp.bfloat16


def two_terms(x):
    high = x.astype(bf16)
    return high, (x - high.astype(f32)).astype(bf16)


def dot(a, b):
    return jnp.dot(a, b, preferred_element_type=f32)


def dot_rows(a, b):
    return lax.dot_general(a, b, (((1,), (1,)), ((), ())), preferred_element_type=f32)


def where_true(rows, cols, test):
    r = lax.broadcasted_iota(jnp.int32, (rows, cols), 0)
    c = lax.broadcasted_iota(jnp.int32, (rows, cols), 1)
    return jnp.where(test(r, c), 1.0, 0.0).astype(f32)


def sine_and_cosine(q):
    y = 0.5 * q
    z = y * y
    s = 0.0
    for n in (11, 9, 7, 5, 3, 1):
        s = s * z + (-1.0) ** (n // 2) / math.factorial(n)
    c = 0.0
    for n in (12, 10, 8, 6, 4, 2, 0):
        c = c * z + (-1.0) ** (n // 2) / math.factorial(n)
    s = s * y
    return 2.0 * s * c, 1.0 - 2.0 * s * s


def body(
    dims,
    x_hbm,
    theta_hbm,
    phi_hbm,
    phase_hbm,
    trans_hbm,
    source_hbm,
    kind_hbm,
    count_hbm,
    out_ref,
    x_ref,
    theta_ref,
    phi_ref,
    phase_ref,
    trans_ref,
    source_ref,
    kind_ref,
    count_ref,
    place_ref,
    index_ref,
    index_sem,
    load_sem,
    cos_ref,
    sin_ref,
    mid_ref,
    turn_ref,
    back_ref,
    spread_lhs,
    spread_rhs,
    fold_lhs,
    fold_rhs,
    table_ref,
    give_ref,
    hold_first,
    hold_second,
    result_ref,
    take_ref,
    give_sem,
    hold_sem,
    pass_sem,
    side_sem,
    result_sem,
    take_sem,
):
    groups, members, coarse_t, coarse_p, fine_t, fine_p, branch, waves, slots, kinds = dims
    pairs = members // 2
    lanes = 2 * fine_p
    columns = branch * waves
    rows8 = waves // 2
    hold = (hold_first, hold_second)
    me = lax.axis_index("mem")
    group = lax.axis_index("grp")
    right = lax.rem(group + 1, groups)
    left = lax.rem(group + groups - 1, groups)

    loads = [
        pltpu.make_async_copy(src, dst, load_sem.at[n])
        for n, (src, dst) in enumerate(
            (
                (x_hbm, x_ref),
                (theta_hbm, theta_ref),
                (phi_hbm, phi_ref),
                (phase_hbm, phase_ref),
                (trans_hbm, trans_ref),
                (source_hbm, source_ref),
                (kind_hbm, kind_ref),
                (count_hbm, count_ref),
            )
        )
    ]
    for load in loads:
        load.start()

    barrier = pltpu.get_barrier_semaphore()

    def greet(k, carry):
        pl.semaphore_signal(
            barrier, inc=1, device_id={"mem": lax.rem(me + k, members)}, device_id_type=MESH
        )
        return carry

    lax.fori_loop(1, members, greet, 0)
    for other in (left, right):
        pl.semaphore_signal(barrier, inc=1, device_id={"grp": other}, device_id_type=MESH)

    def pair_at(k, sign):
        if pairs == 16:
            step = lax.rem(11 * (k + 1), 16)
            home = me // 2
            y = lax.rem(home // 4 + 4 + sign * (step // 4), 4)
            z = lax.rem(lax.rem(home, 4) + 4 + sign * lax.rem(step, 4), 4)
            return 4 * y + z
        return lax.rem(me // 2 + pairs + sign * lax.rem(k + 1, pairs), pairs)

    for load in loads[1:4]:
        load.wait()
    theta_high, theta_low = two_terms(theta_ref[...])
    phi_high, phi_low = two_terms(phi_ref[...])
    at = lambda rows, cols, test: where_true(rows, cols, test).astype(bf16)
    eye = at(fine_t, fine_t, lambda r, c: r == c)
    spread_lhs[...] = (
        dot(dot_rows(eye, theta_high).astype(bf16), at(coarse_t, 3 * coarse_t, lambda r, c: (c == r) | (c == r + coarse_t)))
        + dot(dot_rows(eye, theta_low).astype(bf16), at(coarse_t, 3 * coarse_t, lambda r, c: c == r + 2 * coarse_t))
    ).astype(bf16)
    own = where_true(4 * coarse_p, 4 * fine_p, lambda r, c: r // coarse_p == c // fine_p)
    rows_p = at(4 * coarse_p, coarse_p, lambda r, c: (r & (coarse_p - 1)) == c)
    cols_b = at(fine_p, 4 * fine_p, lambda r, c: r == (c & (fine_p - 1)))
    for n, term in enumerate((phi_high, phi_low)):
        small = dot(rows_p, term).astype(bf16)
        spread_rhs[n] = (dot(small, cols_b) * own).astype(bf16)

    def angles(i, carry):
        at_lanes = pl.ds(pl.multiple_of(i * 2 * lanes, 2 * lanes), 2 * lanes)
        s, c = sine_and_cosine(phase_ref[:, at_lanes])
        sin_ref[:, at_lanes] = s
        cos_ref[:, at_lanes] = c
        return carry

    lax.fori_loop(0, pairs, angles, 0)

    for load in loads[5:]:
        load.wait()

    used = lax.broadcasted_iota(jnp.int32, (slots, members), 0) < count_ref[...]
    place_ref[0] = jnp.where(used, source_ref[...] - (group - 1) * members, members)
    place_ref[1] = jnp.where(used, kind_ref[...], kinds)
    places = pltpu.make_async_copy(place_ref, index_ref, index_sem)
    places.start()

    lhs = spread_lhs[...]
    loads[0].wait()

    def theta_step(p, carry):
        terms = [two_terms(x_ref[n, pl.ds(p, coarse_t, stride=coarse_p), :]) for n in range(2)]
        high = jnp.concatenate([terms[0][0], terms[1][0]], axis=1)
        low = jnp.concatenate([terms[0][1], terms[1][1]], axis=1)
        made = dot(lhs, jnp.concatenate([high, low, high], axis=0))
        for n in range(2):
            mid_ref[n, pl.ds(p, fine_t, stride=coarse_p), :] = made[
                :, n * columns : (n + 1) * columns
            ]
        return carry

    lax.fori_loop(0, coarse_p, theta_step, 0, unroll=8)

    pl.semaphore_wait(barrier, members + 1)

    def give_copy(half, to):
        return pltpu.make_async_remote_copy(
            src_ref=give_ref.at[half, to],
            dst_ref=hold[half].at[members + me],
            send_sem=give_sem.at[half],
            recv_sem=hold_sem.at[half, me // 2],
            device_id={"mem": to},
            device_id_type=MESH,
        )

    def spread_pair(home, k, carry):
        pair = pair_at(k, 1)
        rows = pl.ds(pl.multiple_of(pair * 4 * coarse_p, 4 * coarse_p), 4 * coarse_p)
        turned = jnp.concatenate([mid_ref[0, rows, :].T, mid_ref[1, rows, :].T], axis=0)
        high, low = two_terms(turned)
        both = jnp.concatenate([spread_rhs[0], spread_rhs[0]], axis=0)
        fine = dot(jnp.concatenate([high, low], axis=1), both) + dot(high, spread_rhs[1])
        at_lanes = pl.ds(pl.multiple_of(pair * 2 * lanes, 2 * lanes), 2 * lanes)
        cosine = cos_ref[:, at_lanes]
        sine = sin_ref[:, at_lanes]
        real = imag = 0.0
        for j in range(branch):
            re = fine[j * waves : (j + 1) * waves]
            im = fine[columns + j * waves : columns + (j + 1) * waves]
            c, s = cosine[j : j + 1], sine[j : j + 1]
            real = real + (re * c - im * s)
            imag = imag + (im * c + re * s)
        for side in range(2):
            to = 2 * pair + side
            for half in range(2):
                for n, part in enumerate((real, imag)):
                    give_ref[half, to, n] = part[
                        half * rows8 : (half + 1) * rows8, side * lanes : (side + 1) * lanes
                    ]

            if not home:
                give_copy(0, to).start()
        return carry

    other = me + 1 - 2 * lax.rem(me, 2)
    lax.fori_loop(0, pairs - 1, functools.partial(spread_pair, False), 0, unroll=3)
    spread_pair(True, pairs - 1, 0)
    give_copy(0, other).start()
    for half in range(2):
        hold[half][members + me] = give_ref[half, me]

    def give_rest(k, carry):
        for side in range(2):
            give_copy(1, 2 * pair_at(k, 1) + side).start()
        return carry

    lax.fori_loop(0, pairs - 1, give_rest, 0)
    give_copy(1, other).start()

    loads[4].wait()

    def table_step(i, carry):
        for n in range(2):
            table_ref[i, n] = jnp.broadcast_to(trans_ref[i, pl.ds(n, 1), :], (rows8, lanes))
        return carry

    lax.fori_loop(0, kinds, table_step, 0, unroll=4)
    table_ref[kinds] = jnp.zeros((2, rows8, lanes), f32)

    own_back = where_true(4 * fine_p, 4 * coarse_p, lambda r, c: r // fine_p == c // coarse_p)
    rows_b = at(4 * fine_p, fine_p, lambda r, c: (r & (fine_p - 1)) == c)
    cols_p = at(coarse_p, 4 * coarse_p, lambda r, c: r == (c & (coarse_p - 1)))
    for n, term in enumerate((phi_high, phi_low)):
        small = dot_rows(rows_b, term).astype(bf16)
        fold_rhs[:, n * 4 * coarse_p : (n + 1) * 4 * coarse_p] = (
            dot(small, cols_p) * own_back
        ).astype(bf16)
    fold_lhs[...] = (
        dot(theta_high, at(fine_t, 3 * fine_t, lambda r, c: (c == r) | (c == r + fine_t)))
        + dot(theta_low, at(fine_t, 3 * fine_t, lambda r, c: c == r + 2 * fine_t))
    ).astype(bf16)
    places.wait()

    def pass_copy(half, first, count, way):
        to = right if way == 0 else left
        return pltpu.make_async_remote_copy(
            src_ref=hold[half].at[pl.ds(members + first, count)],
            dst_ref=hold[half].at[pl.ds(2 * members * way + first, count)],
            send_sem=pass_sem.at[half, way],
            recv_sem=side_sem.at[half, way],
            device_id={"grp": to},
            device_id_type=MESH,
        )

    def result_copy(half, target):
        return pltpu.make_async_remote_copy(
            src_ref=result_ref.at[half, target],
            dst_ref=take_ref.at[half, me],
            send_sem=result_sem.at[half],
            recv_sem=take_sem.at[half, me // 2],
            device_id={"mem": target},
            device_id_type=MESH,
        )

    def landed(ref, sem, pair):
        def wait(count):
            pltpu.make_async_remote_copy(
                src_ref=ref.at[pl.ds(0, count)],
                dst_ref=ref.at[pl.ds(0, count)],
                send_sem=give_sem.at[0],
                recv_sem=sem,
                device_id={"mem": other},
                device_id_type=MESH,
            ).wait_recv()

        @pl.when(pair != me // 2)
        def _():
            wait(2)

        @pl.when(pair == me // 2)
        def _():
            wait(1)

    def pass_order(k):
        if pairs == 16:
            return 4 * lax.rem(k, 4) + k // 4
        return k

    for half in range(2):

        def pass_pair(k, carry):
            pair = pass_order(k)
            landed(hold[half].at[pl.ds(members, members)], hold_sem.at[half, pair], pair)
            for way in range(2):
                pass_copy(half, 2 * pair, 2, way).start()
            return carry

        lax.fori_loop(0, pairs, pass_pair, 0)

        for way in range(2):
            span = hold[half].at[pl.ds(2 * members * way, members)]
            pltpu.make_async_remote_copy(
                src_ref=span,
                dst_ref=span,
                send_sem=pass_sem.at[half, way],
                recv_sem=side_sem.at[half, way],
                device_id={"grp": right},
                device_id_type=MESH,
            ).wait_recv()

        def translate(target, away):
            real = jnp.zeros((rows8, lanes), f32)
            imag = jnp.zeros((rows8, lanes), f32)
            for slot in range(slots):
                box = hold[half][index_ref[0, slot, target]]
                factor = table_ref[index_ref[1, slot, target]]
                real = real + (factor[0] * box[0] - factor[1] * box[1])
                imag = imag + (factor[0] * box[1] + factor[1] * box[0])
            if away:
                result_ref[half, target, 0] = real
                result_ref[half, target, 1] = imag
                result_copy(half, target).start()
            else:
                take_ref[half, me, 0] = real
                take_ref[half, me, 1] = imag

        def translate_pair(k, carry):
            for side in range(2):
                translate(2 * pair_at(k, 1) + side, True)
            return carry

        lax.fori_loop(0, pairs - 1, translate_pair, 0)
        translate(other, True)
        translate(me, False)

    width = 4 * coarse_p
    for half in range(2):

        def fold_pair(home, k, carry):
            pair = pair_at(k, -1)
            if home:
                landed(take_ref.at[half], take_sem.at[half, pair], pair)
            else:
                two = take_ref.at[half, pl.ds(0, 2)]
                pltpu.make_async_remote_copy(
                    src_ref=two,
                    dst_ref=two,
                    send_sem=give_sem.at[0],
                    recv_sem=take_sem.at[half, pair],
                    device_id={"mem": other},
                    device_id_type=MESH,
                ).wait_recv()
            at_lanes = pl.ds(pl.multiple_of(pair * 2 * lanes, 2 * lanes), 2 * lanes)
            cosine = cos_ref[:, at_lanes]
            sine = sin_ref[:, at_lanes]
            re, im = (
                jnp.concatenate([take_ref[half, 2 * pair + side, n] for side in range(2)], axis=1)
                for n in range(2)
            )
            parts = [[], []]
            for j in range(branch):
                c, s = cosine[j : j + 1], sine[j : j + 1]
                parts[0].append(re * c + im * s)
                parts[1].append(im * c - re * s)
            high, low = two_terms(jnp.concatenate(parts[0] + parts[1], axis=0))
            wide = dot(high, fold_rhs[...])
            made = wide[:, :width] + wide[:, width:] + dot(low, fold_rhs[:, :width])
            for n in range(2):
                for j in range(branch):
                    first = (n * branch + j) * rows8
                    turn_ref[pair, n, j * waves + half * rows8 : j * waves + (half + 1) * rows8] = (
                        made[first : first + rows8]
                    )
            if half == 1:
                rows = pl.ds(pl.multiple_of(pair * width, width), width)
                for n in range(2):
                    back_ref[n, rows, :] = turn_ref[pair, n].T
            return carry

        fold_pair(True, pairs - 1, 0)
        lax.fori_loop(0, pairs - 1, functools.partial(fold_pair, False), 0, unroll=3)

    lhs_back = fold_lhs[...]

    def fold_step(p, carry):
        terms = [two_terms(back_ref[n, pl.ds(p, fine_t, stride=coarse_p), :]) for n in range(2)]
        high = jnp.concatenate([terms[0][0], terms[1][0]], axis=1)
        low = jnp.concatenate([terms[0][1], terms[1][1]], axis=1)
        made = dot(lhs_back, jnp.concatenate([high, low, high], axis=0))
        for n in range(2):
            out_ref[n, pl.ds(p, coarse_t, stride=coarse_p), :] = made[
                :, n * columns : (n + 1) * columns
            ]
        return carry

    lax.fori_loop(0, coarse_p, fold_step, 0, unroll=8)

    def left_here(ref, sem):
        pltpu.make_async_remote_copy(
            src_ref=ref,
            dst_ref=ref,
            send_sem=sem,
            recv_sem=take_sem.at[0, 0],
            device_id={"mem": other},
            device_id_type=MESH,
        ).wait_send()

    for half in range(2):
        left_here(give_ref.at[half, pl.ds(0, members - 1)], give_sem.at[half])
        left_here(result_ref.at[half, pl.ds(0, members - 1)], result_sem.at[half])
        for way in range(2):
            left_here(hold[half].at[pl.ds(0, members)], pass_sem.at[half, way])


def per_device(groups, members, waves, *arrays):
    field, theta, phi, phase, trans, source, kind, count = arrays
    theta, phi, trans = theta.T, phi.T, trans.transpose(1, 0, 2)
    source, kind, count = source.T, kind.T, count.reshape(1, -1)
    coarse_t, fine_t = theta.shape
    coarse_p, fine_p = phi.shape
    branch = phase.shape[0]
    slots = source.shape[0]
    kinds = trans.shape[0]
    columns = field.shape[2]
    lanes = trans.shape[2]
    dims = (groups, members, coarse_t, coarse_p, fine_t, fine_p, branch, waves, slots, kinds)
    block = (2, waves // 2, lanes)
    return pl.pallas_call(
        functools.partial(body, dims),
        out_shape=jax.ShapeDtypeStruct(field.shape, f32),
        in_specs=[pl.BlockSpec(memory_space=pltpu.HBM)] * 8,
        out_specs=pl.BlockSpec(memory_space=pltpu.VMEM),
        scratch_shapes=[
            *(pltpu.VMEM(a.shape, f32) for a in (field, theta, phi, phase, trans)),
            *(pltpu.VMEM(a.shape, jnp.int32) for a in (source, kind, count)),
            pltpu.VMEM((2, slots, members), jnp.int32),
            pltpu.SMEM((2, slots, members), jnp.int32),
            pltpu.SemaphoreType.DMA,
            pltpu.SemaphoreType.DMA((8,)),
            pltpu.VMEM(phase.shape, f32),
            pltpu.VMEM(phase.shape, f32),
            pltpu.VMEM((2, fine_t * coarse_p, columns), f32),
            pltpu.VMEM((members // 2, 2, columns, 4 * coarse_p), f32),
            pltpu.VMEM((2, fine_t * coarse_p, columns), f32),
            pltpu.VMEM((fine_t, 3 * coarse_t), bf16),
            pltpu.VMEM((2, 4 * coarse_p, 4 * fine_p), bf16),
            pltpu.VMEM((coarse_t, 3 * fine_t), bf16),
            pltpu.VMEM((4 * fine_p, 8 * coarse_p), bf16),
            pltpu.VMEM((kinds + 1, 2, waves // 2, lanes), f32),
            pltpu.VMEM((2, members, *block), f32),
            pltpu.VMEM((3 * members, *block), f32),
            pltpu.VMEM((3 * members, *block), f32),
            pltpu.VMEM((2, members, *block), f32),
            pltpu.VMEM((2, members, *block), f32),
            pltpu.SemaphoreType.DMA((2,)),
            pltpu.SemaphoreType.DMA((2, members // 2)),
            pltpu.SemaphoreType.DMA((2, 2)),
            pltpu.SemaphoreType.DMA((2, 2)),
            pltpu.SemaphoreType.DMA((2,)),
            pltpu.SemaphoreType.DMA((2, members // 2)),
        ],
        compiler_params=pltpu.CompilerParams(
            collective_id=0, has_side_effects=True, vmem_limit_bytes=40 << 20
        ),
    )(*(pltpu.with_memory_space_constraint(a, pltpu.HBM) for a in (field, theta, phi, phase, trans, source, kind, count)))


def solution(mesh):
    groups, members = mesh.shape["grp"], mesh.shape["mem"]

    def run(field, theta, phi, phase, trans, source, kind, count):
        waves = field.shape[2] // phase.shape[0]
        return per_device(
            groups, members, waves, field, theta, phi, phase, trans, source, kind, count
        )

    return jax.shard_map(
        run,
        mesh=mesh,
        in_specs=(
            P(None, None, ("grp", "mem")),
            P(),
            P(),
            P(),
            P(None, None, "mem"),
            P("grp", None),
            P("grp", None),
            P("grp"),
        ),
        out_specs=P(None, None, ("grp", "mem")),
        check_vma=False,
    )
```

```python
import functools
import math

import jax
import jax.numpy as jnp
from jax import lax
from jax.experimental import pallas as pl
from jax.experimental.pallas import tpu as pltpu
from jax.sharding import PartitionSpec as P

MESH = pl.DeviceIdType.MESH
f32 = jnp.float32
bf16 = jnp.bfloat16


def two_terms(x):
    high = x.astype(bf16)
    return high, (x - high.astype(f32)).astype(bf16)


def dot(a, b):
    return jnp.dot(a, b, preferred_element_type=f32)


def dot_rows(a, b):
    return lax.dot_general(a, b, (((1,), (1,)), ((), ())), preferred_element_type=f32)


def where_true(rows, cols, test):
    r = lax.broadcasted_iota(jnp.int32, (rows, cols), 0)
    c = lax.broadcasted_iota(jnp.int32, (rows, cols), 1)
    return jnp.where(test(r, c), 1.0, 0.0).astype(f32)


def sine_and_cosine(q):
    y = 0.5 * q
    z = y * y
    s = 0.0
    for n in (11, 9, 7, 5, 3, 1):
        s = s * z + (-1.0) ** (n // 2) / math.factorial(n)
    c = 0.0
    for n in (12, 10, 8, 6, 4, 2, 0):
        c = c * z + (-1.0) ** (n // 2) / math.factorial(n)
    s = s * y
    return 2.0 * s * c, 1.0 - 2.0 * s * s


def body(
    dims,
    x_hbm,
    theta_hbm,
    phi_hbm,
    phase_hbm,
    trans_hbm,
    source_hbm,
    kind_hbm,
    count_hbm,
    out_ref,
    x_ref,
    theta_ref,
    phi_ref,
    phase_ref,
    trans_ref,
    source_ref,
    kind_ref,
    count_ref,
    place_ref,
    index_ref,
    index_sem,
    load_sem,
    cos_ref,
    sin_ref,
    mid_ref,
    turn_ref,
    back_ref,
    spread_lhs,
    spread_rhs,
    fold_lhs,
    fold_rhs,
    table_ref,
    give_ref,
    hold_0,
    hold_1,
    result_ref,
    take_ref,
    give_sem,
    hold_sem,
    pass_sem,
    side_sem,
    result_sem,
    take_sem,
):
    groups, members, coarse_t, coarse_p, fine_t, fine_p, branch, waves, slots, kinds = dims
    pairs = members // 2
    lanes = 2 * fine_p
    columns = branch * waves
    hold = (hold_0, hold_1)
    chunks = len(hold)
    few = waves // chunks
    half_waves = waves // 2
    chunks_of = lambda half: range(half * chunks // 2, (half + 1) * chunks // 2)
    me = lax.axis_index("mem")
    group = lax.axis_index("grp")
    right = lax.rem(group + 1, groups)
    left = lax.rem(group + groups - 1, groups)

    loads = [
        pltpu.make_async_copy(src, dst, load_sem.at[n])
        for n, (src, dst) in enumerate(
            (
                (x_hbm, x_ref),
                (theta_hbm, theta_ref),
                (phi_hbm, phi_ref),
                (phase_hbm, phase_ref),
                (trans_hbm, trans_ref),
                (source_hbm, source_ref),
                (kind_hbm, kind_ref),
                (count_hbm, count_ref),
            )
        )
    ]
    for load in loads:
        load.start()

    barrier = pltpu.get_barrier_semaphore()

    def greet(k, carry):
        pl.semaphore_signal(
            barrier, inc=1, device_id={"mem": lax.rem(me + k, members)}, device_id_type=MESH
        )
        return carry

    lax.fori_loop(1, members, greet, 0)
    for other in (left, right):
        pl.semaphore_signal(barrier, inc=1, device_id={"grp": other}, device_id_type=MESH)

    home_pair = me // 2
    row = members // 4

    def pair_at(k, sign):
        if sign == 1:
            up = home_pair + (k + 1)
            return jnp.where(up >= pairs, up - pairs, up)
        down = home_pair - (k + 1)
        return jnp.where(down < 0, down + pairs, down)

    for load in loads[1:4]:
        load.wait()
    theta_high, theta_low = two_terms(theta_ref[...])
    phi_high, phi_low = two_terms(phi_ref[...])
    at = lambda rows, cols, test: where_true(rows, cols, test).astype(bf16)
    eye = at(fine_t, fine_t, lambda r, c: r == c)
    spread_lhs[...] = (
        dot(dot_rows(eye, theta_high).astype(bf16), at(coarse_t, 3 * coarse_t, lambda r, c: (c == r) | (c == r + coarse_t)))
        + dot(dot_rows(eye, theta_low).astype(bf16), at(coarse_t, 3 * coarse_t, lambda r, c: c == r + 2 * coarse_t))
    ).astype(bf16)
    own = where_true(4 * coarse_p, 4 * fine_p, lambda r, c: r // coarse_p == c // fine_p)
    rows_p = at(4 * coarse_p, coarse_p, lambda r, c: (r & (coarse_p - 1)) == c)
    cols_b = at(fine_p, 4 * fine_p, lambda r, c: r == (c & (fine_p - 1)))
    for n, term in enumerate((phi_high, phi_low)):
        small = dot(rows_p, term).astype(bf16)
        spread_rhs[n] = (dot(small, cols_b) * own).astype(bf16)

    def angles(i, carry):
        at_lanes = pl.ds(pl.multiple_of(i * 2 * lanes, 2 * lanes), 2 * lanes)
        s, c = sine_and_cosine(phase_ref[:, at_lanes])
        sin_ref[:, at_lanes] = s
        cos_ref[:, at_lanes] = c
        return carry

    lax.fori_loop(0, pairs, angles, 0)

    for load in loads[5:]:
        load.wait()

    used = lax.broadcasted_iota(jnp.int32, (slots, members), 0) < count_ref[...]
    place_ref[0] = jnp.where(used, source_ref[...] - (group - 1) * members, members)
    place_ref[1] = jnp.where(used, kind_ref[...], kinds)
    places = pltpu.make_async_copy(place_ref, index_ref, index_sem)
    places.start()

    lhs = spread_lhs[...]
    loads[0].wait()

    def theta_step(p, carry):
        terms = [two_terms(x_ref[n, pl.ds(p, coarse_t, stride=coarse_p), :]) for n in range(2)]
        high = jnp.concatenate([terms[0][0], terms[1][0]], axis=1)
        low = jnp.concatenate([terms[0][1], terms[1][1]], axis=1)
        made = dot(lhs, jnp.concatenate([high, low, high], axis=0))
        for n in range(2):
            mid_ref[n, pl.ds(p, fine_t, stride=coarse_p), :] = made[
                :, n * columns : (n + 1) * columns
            ]
        return carry

    lax.fori_loop(0, coarse_p, theta_step, 0, unroll=32)

    pl.semaphore_wait(barrier, members + 1)

    def give_copy(half, to):
        return pltpu.make_async_remote_copy(
            src_ref=give_ref.at[half, to],
            dst_ref=hold[half].at[members + me],
            send_sem=give_sem.at[half],
            recv_sem=hold_sem.at[half, me // row],
            device_id={"mem": to},
            device_id_type=MESH,
        )

    def spread_pair(home, k, carry):
        pair = pair_at(k, 1)
        rows = pl.ds(pl.multiple_of(pair * 4 * coarse_p, 4 * coarse_p), 4 * coarse_p)
        turned = jnp.concatenate([mid_ref[0, rows, :].T, mid_ref[1, rows, :].T], axis=0)
        high, low = two_terms(turned)
        both = jnp.concatenate([spread_rhs[0], spread_rhs[0]], axis=0)
        fine = dot(jnp.concatenate([high, low], axis=1), both) + dot(high, spread_rhs[1])
        at_lanes = pl.ds(pl.multiple_of(pair * 2 * lanes, 2 * lanes), 2 * lanes)
        cosine = cos_ref[:, at_lanes]
        sine = sin_ref[:, at_lanes]
        real = imag = 0.0
        for j in range(branch):
            re = fine[j * waves : (j + 1) * waves]
            im = fine[columns + j * waves : columns + (j + 1) * waves]
            c, s = cosine[j : j + 1], sine[j : j + 1]
            real = real + (re * c - im * s)
            imag = imag + (im * c + re * s)
        for side in range(2):
            to = 2 * pair + side
            for chunk in range(chunks):
                give_ref[chunk, to] = jnp.concatenate(
                    [
                        part[chunk * few : (chunk + 1) * few, side * lanes : (side + 1) * lanes]
                        for part in (real, imag)
                    ],
                    axis=0,
                )

            if not home:
                give_copy(0, to).start()
        return carry

    other = me + 1 - 2 * lax.rem(me, 2)
    lax.fori_loop(0, pairs - 1, functools.partial(spread_pair, False), 0, unroll=3)
    spread_pair(True, pairs - 1, 0)
    give_copy(0, other).start()
    for chunk in range(chunks):
        hold[chunk][members + me] = give_ref[chunk, me]

    for chunk in range(1, chunks):

        def give_rest(k, carry):
            for side in range(2):
                give_copy(chunk, 2 * pair_at(k, 1) + side).start()
            return carry

        lax.fori_loop(0, pairs - 1, give_rest, 0)
        give_copy(chunk, other).start()

    loads[4].wait()

    signs = jnp.where(lax.broadcasted_iota(jnp.int32, (2 * few, lanes), 0) < few, 1.0, -1.0)

    def table_step(i, carry):
        for n in range(2):
            row = jnp.broadcast_to(trans_ref[i, pl.ds(n, 1), :], (2 * few, lanes))
            table_ref[i, n] = row if n == 0 else row * signs
        return carry

    lax.fori_loop(0, kinds, table_step, 0, unroll=4)
    table_ref[kinds] = jnp.zeros((2, 2 * few, lanes), f32)

    own_back = where_true(4 * fine_p, 4 * coarse_p, lambda r, c: r // fine_p == c // coarse_p)
    rows_b = at(4 * fine_p, fine_p, lambda r, c: (r & (fine_p - 1)) == c)
    cols_p = at(coarse_p, 4 * coarse_p, lambda r, c: r == (c & (coarse_p - 1)))
    for n, term in enumerate((phi_high, phi_low)):
        small = dot_rows(rows_b, term).astype(bf16)
        fold_rhs[:, n * 4 * coarse_p : (n + 1) * 4 * coarse_p] = (
            dot(small, cols_p) * own_back
        ).astype(bf16)
    fold_lhs[...] = (
        dot(theta_high, at(fine_t, 3 * fine_t, lambda r, c: (c == r) | (c == r + fine_t)))
        + dot(theta_low, at(fine_t, 3 * fine_t, lambda r, c: c == r + 2 * fine_t))
    ).astype(bf16)
    places.wait()

    def pass_copy(half, first, count, way):
        to = right if way == 0 else left
        return pltpu.make_async_remote_copy(
            src_ref=hold[half].at[pl.ds(members + first, count)],
            dst_ref=hold[half].at[pl.ds(2 * members * way + first, count)],
            send_sem=pass_sem.at[half, way],
            recv_sem=side_sem.at[half, way],
            device_id={"grp": to},
            device_id_type=MESH,
        )

    def result_copy(half, target):
        return pltpu.make_async_remote_copy(
            src_ref=result_ref.at[half, target],
            dst_ref=take_ref.at[half, me],
            send_sem=result_sem.at[half],
            recv_sem=take_sem.at[half, me // 2 if half == chunks - 1 else 0],
            device_id={"mem": target},
            device_id_type=MESH,
        )

    def blocks_landed(ref, sem, count):
        some = ref.at[pl.ds(0, count)]
        pltpu.make_async_remote_copy(
            src_ref=some,
            dst_ref=some,
            send_sem=give_sem.at[0],
            recv_sem=sem,
            device_id={"mem": other},
            device_id_type=MESH,
        ).wait_recv()

    def pass_row(half, k, carry):
        @pl.when(k == me // row)
        def _():
            blocks_landed(hold[half], hold_sem.at[half, k], row - 1)

        @pl.when(k != me // row)
        def _():
            blocks_landed(hold[half], hold_sem.at[half, k], row)

        for way in range(2):
            pass_copy(half, row * k, row, way).start()
        return carry

    def sides_landed(half):
        for way in range(2):
            span = hold[half].at[pl.ds(2 * members * way, members)]
            pltpu.make_async_remote_copy(
                src_ref=span,
                dst_ref=span,
                send_sem=pass_sem.at[half, way],
                recv_sem=side_sem.at[half, way],
                device_id={"grp": right},
                device_id_type=MESH,
            ).wait_recv()

    def translate(half, target, away):
        straight = jnp.zeros((2 * few, lanes), f32)
        crossed = jnp.zeros((2 * few, lanes), f32)
        for slot in range(slots):
            box = hold[half][index_ref[0, slot, target]]
            factor = table_ref[index_ref[1, slot, target]]
            straight = straight + factor[0] * box
            crossed = crossed + factor[1] * box
        made = straight + jnp.concatenate([crossed[few:], crossed[:few]], axis=0)
        if away:
            result_ref[half, target] = made
            result_copy(half, target).start()
        else:
            take_ref[half, me] = made

    def translate_pair(half, k, carry):
        for side in range(2):
            translate(half, 2 * pair_at(k, 1) + side, True)
        return carry

    def pass_rows(chunk, first, end):
        lax.fori_loop(first, end, functools.partial(pass_row, chunk), 0)

    def translate_all(chunk):
        lax.fori_loop(0, pairs - 1, functools.partial(translate_pair, chunk), 0)
        translate(chunk, other, True)
        translate(chunk, me, False)

    rows = members // row
    pass_rows(0, 0, rows)
    pass_rows(1, 0, rows - 1)
    sides_landed(0)
    translate_all(0)
    pass_rows(1, rows - 1, rows)
    sides_landed(1)
    translate_all(1)

    width = 4 * coarse_p
    for half in range(2):

        def fold_pair(home, k, carry):
            pair = pair_at(k, -1)
            if half == 1:
                last = chunks - 1
                blocks_landed(take_ref.at[last], take_sem.at[last, pair], 1 if home else 2)
            at_lanes = pl.ds(pl.multiple_of(pair * 2 * lanes, 2 * lanes), 2 * lanes)
            cosine = cos_ref[:, at_lanes]
            sine = sin_ref[:, at_lanes]
            re, im = (
                jnp.concatenate(
                    [
                        jnp.concatenate(
                            [
                                take_ref[chunk, 2 * pair + side, n * few : (n + 1) * few]
                                for chunk in chunks_of(half)
                            ],
                            axis=0,
                        )
                        for side in range(2)
                    ],
                    axis=1,
                )
                for n in range(2)
            )
            parts = [[], []]
            for j in range(branch):
                c, s = cosine[j : j + 1], sine[j : j + 1]
                parts[0].append(re * c + im * s)
                parts[1].append(im * c - re * s)
            high, low = two_terms(jnp.concatenate(parts[0] + parts[1], axis=0))
            wide = dot(high, fold_rhs[...])
            made = wide[:, :width] + wide[:, width:] + dot(low, fold_rhs[:, :width])
            for n in range(2):
                for j in range(branch):
                    first = (n * branch + j) * half_waves
                    to = j * waves + half * half_waves
                    turn_ref[pair, n, to : to + half_waves] = made[first : first + half_waves]
            if half == 1:
                rows = pl.ds(pl.multiple_of(pair * width, width), width)
                for n in range(2):
                    back_ref[n, rows, :] = turn_ref[pair, n].T
            return carry

        for chunk in chunks_of(half):
            if chunk < chunks - 1:
                blocks_landed(take_ref.at[chunk], take_sem.at[chunk, 0], members - 1)
        lax.fori_loop(0, pairs - 1, functools.partial(fold_pair, False), 0, unroll=3)
        fold_pair(True, pairs - 1, 0)

    lhs_back = fold_lhs[...]

    def fold_step(p, carry):
        terms = [two_terms(back_ref[n, pl.ds(p, fine_t, stride=coarse_p), :]) for n in range(2)]
        high = jnp.concatenate([terms[0][0], terms[1][0]], axis=1)
        low = jnp.concatenate([terms[0][1], terms[1][1]], axis=1)
        made = dot(lhs_back, jnp.concatenate([high, low, high], axis=0))
        for n in range(2):
            out_ref[n, pl.ds(p, coarse_t, stride=coarse_p), :] = made[
                :, n * columns : (n + 1) * columns
            ]
        return carry

    lax.fori_loop(0, coarse_p, fold_step, 0, unroll=32)

    def left_here(ref, sem):
        pltpu.make_async_remote_copy(
            src_ref=ref,
            dst_ref=ref,
            send_sem=sem,
            recv_sem=take_sem.at[0, 0],
            device_id={"mem": other},
            device_id_type=MESH,
        ).wait_send()

    for half in range(chunks):
        left_here(give_ref.at[half, pl.ds(0, members - 1)], give_sem.at[half])
        left_here(result_ref.at[half, pl.ds(0, members - 1)], result_sem.at[half])
        for way in range(2):
            left_here(hold[half].at[pl.ds(0, members)], pass_sem.at[half, way])


def per_device(groups, members, waves, *arrays):
    field, theta, phi, phase, trans, source, kind, count = arrays
    theta, phi, trans = theta.T, phi.T, trans.transpose(1, 0, 2)
    source, kind, count = source.T, kind.T, count.reshape(1, -1)
    coarse_t, fine_t = theta.shape
    coarse_p, fine_p = phi.shape
    branch = phase.shape[0]
    slots = source.shape[0]
    kinds = trans.shape[0]
    columns = field.shape[2]
    lanes = trans.shape[2]
    dims = (groups, members, coarse_t, coarse_p, fine_t, fine_p, branch, waves, slots, kinds)
    chunks = 2
    block = (2 * (waves // chunks), lanes)
    return pl.pallas_call(
        functools.partial(body, dims),
        out_shape=jax.ShapeDtypeStruct(field.shape, f32),
        in_specs=[pl.BlockSpec(memory_space=pltpu.HBM)] * 8,
        out_specs=pl.BlockSpec(memory_space=pltpu.VMEM),
        scratch_shapes=[
            *(pltpu.VMEM(a.shape, f32) for a in (field, theta, phi, phase, trans)),
            *(pltpu.VMEM(a.shape, jnp.int32) for a in (source, kind, count)),
            pltpu.VMEM((2, slots, members), jnp.int32),
            pltpu.SMEM((2, slots, members), jnp.int32),
            pltpu.SemaphoreType.DMA,
            pltpu.SemaphoreType.DMA((8,)),
            pltpu.VMEM(phase.shape, f32),
            pltpu.VMEM(phase.shape, f32),
            pltpu.VMEM((2, fine_t * coarse_p, columns), f32),
            pltpu.VMEM((members // 2, 2, columns, 4 * coarse_p), f32),
            pltpu.VMEM((2, fine_t * coarse_p, columns), f32),
            pltpu.VMEM((fine_t, 3 * coarse_t), bf16),
            pltpu.VMEM((2, 4 * coarse_p, 4 * fine_p), bf16),
            pltpu.VMEM((coarse_t, 3 * fine_t), bf16),
            pltpu.VMEM((4 * fine_p, 8 * coarse_p), bf16),
            pltpu.VMEM((kinds + 1, 2, *block), f32),
            pltpu.VMEM((chunks, members, *block), f32),
            *(pltpu.VMEM((3 * members, *block), f32) for _ in range(chunks)),
            pltpu.VMEM((chunks, members, *block), f32),
            pltpu.VMEM((chunks, members, *block), f32),
            pltpu.SemaphoreType.DMA((chunks,)),
            pltpu.SemaphoreType.DMA((chunks, 4)),
            pltpu.SemaphoreType.DMA((chunks, 2)),
            pltpu.SemaphoreType.DMA((chunks, 2)),
            pltpu.SemaphoreType.DMA((chunks,)),
            pltpu.SemaphoreType.DMA((chunks, members // 2)),
        ],
        compiler_params=pltpu.CompilerParams(
            collective_id=0, has_side_effects=True, vmem_limit_bytes=40 << 20
        ),
    )(*(pltpu.with_memory_space_constraint(a, pltpu.HBM) for a in (field, theta, phi, phase, trans, source, kind, count)))


def solution(mesh):
    groups, members = mesh.shape["grp"], mesh.shape["mem"]

    def run(field, theta, phi, phase, trans, source, kind, count):
        waves = field.shape[2] // phase.shape[0]
        return per_device(
            groups, members, waves, field, theta, phi, phase, trans, source, kind, count
        )

    return jax.shard_map(
        run,
        mesh=mesh,
        in_specs=(
            P(None, None, ("grp", "mem")),
            P(),
            P(),
            P(),
            P(None, None, "mem"),
            P("grp", None),
            P("grp", None),
            P("grp"),
        ),
        out_specs=P(None, None, ("grp", "mem")),
        check_vma=False,
    )
```

```python
import functools
import math

import jax
import jax.numpy as jnp
from jax import lax
from jax.experimental import pallas as pl
from jax.experimental.pallas import tpu as pltpu
from jax.sharding import PartitionSpec as P

MESH = pl.DeviceIdType.MESH
f32 = jnp.float32
bf16 = jnp.bfloat16


def two_terms(x):
    high = x.astype(bf16)
    return high, (x - high.astype(f32)).astype(bf16)


def dot(a, b):
    return jnp.dot(a, b, preferred_element_type=f32)


def dot_rows(a, b):
    return lax.dot_general(a, b, (((1,), (1,)), ((), ())), preferred_element_type=f32)


def where_true(rows, cols, test):
    r = lax.broadcasted_iota(jnp.int32, (rows, cols), 0)
    c = lax.broadcasted_iota(jnp.int32, (rows, cols), 1)
    return jnp.where(test(r, c), 1.0, 0.0).astype(f32)


def sine_and_cosine(q):
    y = 0.5 * q
    z = y * y
    s = 0.0
    for n in (11, 9, 7, 5, 3, 1):
        s = s * z + (-1.0) ** (n // 2) / math.factorial(n)
    c = 0.0
    for n in (12, 10, 8, 6, 4, 2, 0):
        c = c * z + (-1.0) ** (n // 2) / math.factorial(n)
    s = s * y
    return 2.0 * s * c, 1.0 - 2.0 * s * s


def body(
    dims,
    x_hbm,
    theta_hbm,
    phi_hbm,
    phase_hbm,
    trans_hbm,
    source_hbm,
    kind_hbm,
    count_hbm,
    out_ref,
    x_ref,
    theta_ref,
    phi_ref,
    phase_ref,
    trans_ref,
    source_ref,
    kind_ref,
    count_ref,
    place_ref,
    index_ref,
    index_sem,
    load_sem,
    cos_ref,
    sin_ref,
    mid_ref,
    turn_ref,
    back_ref,
    spread_lhs,
    spread_rhs,
    fold_lhs,
    fold_rhs,
    table_ref,
    give_ref,
    hold_0,
    hold_1,
    result_ref,
    take_ref,
    give_sem,
    hold_sem,
    pass_sem,
    side_sem,
    result_sem,
    take_sem,
):
    groups, members, coarse_t, coarse_p, fine_t, fine_p, branch, waves, slots, kinds = dims
    pairs = members // 2
    lanes = 2 * fine_p
    columns = branch * waves
    hold = (hold_0, hold_1)
    chunks = len(hold)
    few = waves // chunks
    half_waves = waves // 2
    chunks_of = lambda half: range(half * chunks // 2, (half + 1) * chunks // 2)
    me = lax.axis_index("mem")
    group = lax.axis_index("grp")
    right = lax.rem(group + 1, groups)
    left = lax.rem(group + groups - 1, groups)

    loads = [
        pltpu.make_async_copy(src, dst, load_sem.at[n])
        for n, (src, dst) in enumerate(
            (
                (x_hbm, x_ref),
                (theta_hbm, theta_ref),
                (phi_hbm, phi_ref),
                (phase_hbm, phase_ref),
                (trans_hbm, trans_ref),
                (source_hbm, source_ref),
                (kind_hbm, kind_ref),
                (count_hbm, count_ref),
            )
        )
    ]
    for load in loads:
        load.start()

    barrier = pltpu.get_barrier_semaphore()

    def greet(k, carry):
        pl.semaphore_signal(
            barrier, inc=1, device_id={"mem": lax.rem(me + k, members)}, device_id_type=MESH
        )
        return carry

    lax.fori_loop(1, members, greet, 0)
    for other in (left, right):
        pl.semaphore_signal(barrier, inc=1, device_id={"grp": other}, device_id_type=MESH)

    home_pair = me // 2
    row = members // 4

    def pair_at(k, sign):
        if sign == 1:
            up = home_pair + (k + 1)
            return jnp.where(up >= pairs, up - pairs, up)
        down = home_pair - (k + 1)
        return jnp.where(down < 0, down + pairs, down)

    for load in loads[1:4]:
        load.wait()
    theta_high, theta_low = two_terms(theta_ref[...])
    phi_high, phi_low = two_terms(phi_ref[...])
    at = lambda rows, cols, test: where_true(rows, cols, test).astype(bf16)
    eye = at(fine_t, fine_t, lambda r, c: r == c)
    spread_lhs[...] = (
        dot(dot_rows(eye, theta_high).astype(bf16), at(coarse_t, 3 * coarse_t, lambda r, c: (c == r) | (c == r + coarse_t)))
        + dot(dot_rows(eye, theta_low).astype(bf16), at(coarse_t, 3 * coarse_t, lambda r, c: c == r + 2 * coarse_t))
    ).astype(bf16)
    own = where_true(4 * coarse_p, 4 * fine_p, lambda r, c: r // coarse_p == c // fine_p)
    rows_p = at(4 * coarse_p, coarse_p, lambda r, c: (r & (coarse_p - 1)) == c)
    cols_b = at(fine_p, 4 * fine_p, lambda r, c: r == (c & (fine_p - 1)))
    for n, term in enumerate((phi_high, phi_low)):
        small = dot(rows_p, term).astype(bf16)
        spread_rhs[n] = (dot(small, cols_b) * own).astype(bf16)

    def angles(i, carry):
        at_lanes = pl.ds(pl.multiple_of(i * 2 * lanes, 2 * lanes), 2 * lanes)
        s, c = sine_and_cosine(phase_ref[:, at_lanes])
        sin_ref[:, at_lanes] = s
        cos_ref[:, at_lanes] = c
        return carry

    lax.fori_loop(0, pairs, angles, 0)

    lhs = spread_lhs[...]
    loads[0].wait()

    def theta_step(p, carry):
        terms = [two_terms(x_ref[n, pl.ds(p, coarse_t, stride=coarse_p), :]) for n in range(2)]
        high = jnp.concatenate([terms[0][0], terms[1][0]], axis=1)
        low = jnp.concatenate([terms[0][1], terms[1][1]], axis=1)
        made = dot(lhs, jnp.concatenate([high, low, high], axis=0))
        for n in range(2):
            mid_ref[n, pl.ds(p, fine_t, stride=coarse_p), :] = made[
                :, n * columns : (n + 1) * columns
            ]
        return carry

    lax.fori_loop(0, coarse_p, theta_step, 0, unroll=32)

    pl.semaphore_wait(barrier, members + 1)

    def give_copy(half, to):
        return pltpu.make_async_remote_copy(
            src_ref=give_ref.at[half, to],
            dst_ref=hold[half].at[members + me],
            send_sem=give_sem.at[half],
            recv_sem=hold_sem.at[half, me // row],
            device_id={"mem": to},
            device_id_type=MESH,
        )

    def spread_pair(home, k, carry):
        pair = pair_at(k, 1)
        rows = pl.ds(pl.multiple_of(pair * 4 * coarse_p, 4 * coarse_p), 4 * coarse_p)
        turned = jnp.concatenate([mid_ref[0, rows, :].T, mid_ref[1, rows, :].T], axis=0)
        high, low = two_terms(turned)
        both = jnp.concatenate([spread_rhs[0], spread_rhs[0]], axis=0)
        fine = dot(jnp.concatenate([high, low], axis=1), both) + dot(high, spread_rhs[1])
        at_lanes = pl.ds(pl.multiple_of(pair * 2 * lanes, 2 * lanes), 2 * lanes)
        cosine = cos_ref[:, at_lanes]
        sine = sin_ref[:, at_lanes]
        real = imag = 0.0
        for j in range(branch):
            re = fine[j * waves : (j + 1) * waves]
            im = fine[columns + j * waves : columns + (j + 1) * waves]
            c, s = cosine[j : j + 1], sine[j : j + 1]
            real = real + (re * c - im * s)
            imag = imag + (im * c + re * s)
        for side in range(2):
            to = 2 * pair + side
            for chunk in range(chunks):
                give_ref[chunk, to] = jnp.concatenate(
                    [
                        part[chunk * few : (chunk + 1) * few, side * lanes : (side + 1) * lanes]
                        for part in (real, imag)
                    ],
                    axis=0,
                )

            if not home:
                give_copy(0, to).start()
        return carry

    other = me + 1 - 2 * lax.rem(me, 2)
    lax.fori_loop(0, pairs - 1, functools.partial(spread_pair, False), 0, unroll=3)
    spread_pair(True, pairs - 1, 0)
    give_copy(0, other).start()
    for chunk in range(chunks):
        hold[chunk][members + me] = give_ref[chunk, me]

    for chunk in range(1, chunks):

        def give_rest(k, carry):
            for side in range(2):
                give_copy(chunk, 2 * pair_at(k, 1) + side).start()
            return carry

        lax.fori_loop(0, pairs - 1, give_rest, 0)
        give_copy(chunk, other).start()

    for load in loads[5:]:
        load.wait()

    used = lax.broadcasted_iota(jnp.int32, (slots, members), 0) < count_ref[...]
    place_ref[0] = jnp.where(used, source_ref[...] - (group - 1) * members, members)
    place_ref[1] = jnp.where(used, kind_ref[...], kinds)
    places = pltpu.make_async_copy(place_ref, index_ref, index_sem)
    places.start()

    loads[4].wait()

    signs = jnp.where(lax.broadcasted_iota(jnp.int32, (2 * few, lanes), 0) < few, 1.0, -1.0)

    def table_step(i, carry):
        for n in range(2):
            row = jnp.broadcast_to(trans_ref[i, pl.ds(n, 1), :], (2 * few, lanes))
            table_ref[i, n] = row if n == 0 else row * signs
        return carry

    lax.fori_loop(0, kinds, table_step, 0, unroll=4)
    table_ref[kinds] = jnp.zeros((2, 2 * few, lanes), f32)

    own_back = where_true(4 * fine_p, 4 * coarse_p, lambda r, c: r // fine_p == c // coarse_p)
    rows_b = at(4 * fine_p, fine_p, lambda r, c: (r & (fine_p - 1)) == c)
    cols_p = at(coarse_p, 4 * coarse_p, lambda r, c: r == (c & (coarse_p - 1)))
    for n, term in enumerate((phi_high, phi_low)):
        small = dot_rows(rows_b, term).astype(bf16)
        fold_rhs[:, n * 4 * coarse_p : (n + 1) * 4 * coarse_p] = (
            dot(small, cols_p) * own_back
        ).astype(bf16)
    fold_lhs[...] = (
        dot(theta_high, at(fine_t, 3 * fine_t, lambda r, c: (c == r) | (c == r + fine_t)))
        + dot(theta_low, at(fine_t, 3 * fine_t, lambda r, c: c == r + 2 * fine_t))
    ).astype(bf16)
    places.wait()

    def pass_copy(half, first, count, way):
        to = right if way == 0 else left
        return pltpu.make_async_remote_copy(
            src_ref=hold[half].at[pl.ds(members + first, count)],
            dst_ref=hold[half].at[pl.ds(2 * members * way + first, count)],
            send_sem=pass_sem.at[half, way],
            recv_sem=side_sem.at[half, way],
            device_id={"grp": to},
            device_id_type=MESH,
        )

    def result_copy(half, target):
        return pltpu.make_async_remote_copy(
            src_ref=result_ref.at[half, target],
            dst_ref=take_ref.at[half, me],
            send_sem=result_sem.at[half],
            recv_sem=take_sem.at[half, me // 2 if half == chunks - 1 else 0],
            device_id={"mem": target},
            device_id_type=MESH,
        )

    def blocks_landed(ref, sem, count):
        some = ref.at[pl.ds(0, count)]
        pltpu.make_async_remote_copy(
            src_ref=some,
            dst_ref=some,
            send_sem=give_sem.at[0],
            recv_sem=sem,
            device_id={"mem": other},
            device_id_type=MESH,
        ).wait_recv()

    def pass_row(half, k, carry):
        @pl.when(k == me // row)
        def _():
            blocks_landed(hold[half], hold_sem.at[half, k], row - 1)

        @pl.when(k != me // row)
        def _():
            blocks_landed(hold[half], hold_sem.at[half, k], row)

        for way in range(2):
            pass_copy(half, row * k, row, way).start()
        return carry

    def sides_landed(half):
        for way in range(2):
            span = hold[half].at[pl.ds(2 * members * way, members)]
            pltpu.make_async_remote_copy(
                src_ref=span,
                dst_ref=span,
                send_sem=pass_sem.at[half, way],
                recv_sem=side_sem.at[half, way],
                device_id={"grp": right},
                device_id_type=MESH,
            ).wait_recv()

    def translate(half, target, away):
        straight = jnp.zeros((2 * few, lanes), f32)
        crossed = jnp.zeros((2 * few, lanes), f32)
        for slot in range(slots):
            box = hold[half][index_ref[0, slot, target]]
            factor = table_ref[index_ref[1, slot, target]]
            straight = straight + factor[0] * box
            crossed = crossed + factor[1] * box
        made = straight + jnp.concatenate([crossed[few:], crossed[:few]], axis=0)
        if away:
            result_ref[half, target] = made
            result_copy(half, target).start()
        else:
            take_ref[half, me] = made

    def translate_pair(half, k, carry):
        for side in range(2):
            translate(half, 2 * pair_at(k, 1) + side, True)
        return carry

    def pass_rows(chunk, first, end):
        lax.fori_loop(first, end, functools.partial(pass_row, chunk), 0)

    def translate_all(chunk):
        lax.fori_loop(0, pairs - 1, functools.partial(translate_pair, chunk), 0, unroll=3)
        translate(chunk, other, True)
        translate(chunk, me, False)

    rows = members // row
    pass_rows(0, 0, rows)
    pass_rows(1, 0, rows - 1)
    sides_landed(0)
    translate_all(0)
    pass_rows(1, rows - 1, rows)
    sides_landed(1)
    translate_all(1)

    width = 4 * coarse_p
    for half in range(2):

        def fold_pair(home, k, carry):
            pair = pair_at(k, -1)
            if half == 1:
                last = chunks - 1
                blocks_landed(take_ref.at[last], take_sem.at[last, pair], 1 if home else 2)
            at_lanes = pl.ds(pl.multiple_of(pair * 2 * lanes, 2 * lanes), 2 * lanes)
            cosine = cos_ref[:, at_lanes]
            sine = sin_ref[:, at_lanes]
            re, im = (
                jnp.concatenate(
                    [
                        jnp.concatenate(
                            [
                                take_ref[chunk, 2 * pair + side, n * few : (n + 1) * few]
                                for chunk in chunks_of(half)
                            ],
                            axis=0,
                        )
                        for side in range(2)
                    ],
                    axis=1,
                )
                for n in range(2)
            )
            parts = [[], []]
            for j in range(branch):
                c, s = cosine[j : j + 1], sine[j : j + 1]
                parts[0].append(re * c + im * s)
                parts[1].append(im * c - re * s)
            high, low = two_terms(jnp.concatenate(parts[0] + parts[1], axis=0))
            wide = dot(high, fold_rhs[...])
            made = wide[:, :width] + wide[:, width:] + dot(low, fold_rhs[:, :width])
            for n in range(2):
                for j in range(branch):
                    first = (n * branch + j) * half_waves
                    to = j * waves + half * half_waves
                    turn_ref[pair, n, to : to + half_waves] = made[first : first + half_waves]
            if half == 1:
                rows = pl.ds(pl.multiple_of(pair * width, width), width)
                for n in range(2):
                    back_ref[n, rows, :] = turn_ref[pair, n].T
            return carry

        for chunk in chunks_of(half):
            if chunk < chunks - 1:
                blocks_landed(take_ref.at[chunk], take_sem.at[chunk, 0], members - 1)
        lax.fori_loop(0, pairs - 1, functools.partial(fold_pair, False), 0, unroll=5)
        fold_pair(True, pairs - 1, 0)

    lhs_back = fold_lhs[...]

    def fold_step(p, carry):
        terms = [two_terms(back_ref[n, pl.ds(p, fine_t, stride=coarse_p), :]) for n in range(2)]
        high = jnp.concatenate([terms[0][0], terms[1][0]], axis=1)
        low = jnp.concatenate([terms[0][1], terms[1][1]], axis=1)
        made = dot(lhs_back, jnp.concatenate([high, low, high], axis=0))
        for n in range(2):
            out_ref[n, pl.ds(p, coarse_t, stride=coarse_p), :] = made[
                :, n * columns : (n + 1) * columns
            ]
        return carry

    lax.fori_loop(0, coarse_p, fold_step, 0, unroll=32)

    def left_here(ref, sem):
        pltpu.make_async_remote_copy(
            src_ref=ref,
            dst_ref=ref,
            send_sem=sem,
            recv_sem=take_sem.at[0, 0],
            device_id={"mem": other},
            device_id_type=MESH,
        ).wait_send()

    for half in range(chunks):
        left_here(give_ref.at[half, pl.ds(0, members - 1)], give_sem.at[half])
        left_here(result_ref.at[half, pl.ds(0, members - 1)], result_sem.at[half])
        for way in range(2):
            left_here(hold[half].at[pl.ds(0, members)], pass_sem.at[half, way])


def per_device(groups, members, waves, *arrays):
    field, theta, phi, phase, trans, source, kind, count = arrays
    theta, phi, trans = theta.T, phi.T, trans.transpose(1, 0, 2)
    source, kind, count = source.T, kind.T, count.reshape(1, -1)
    coarse_t, fine_t = theta.shape
    coarse_p, fine_p = phi.shape
    branch = phase.shape[0]
    slots = source.shape[0]
    kinds = trans.shape[0]
    columns = field.shape[2]
    lanes = trans.shape[2]
    dims = (groups, members, coarse_t, coarse_p, fine_t, fine_p, branch, waves, slots, kinds)
    chunks = 2
    block = (2 * (waves // chunks), lanes)
    return pl.pallas_call(
        functools.partial(body, dims),
        out_shape=jax.ShapeDtypeStruct(field.shape, f32),
        in_specs=[pl.BlockSpec(memory_space=pltpu.HBM)] * 8,
        out_specs=pl.BlockSpec(memory_space=pltpu.VMEM),
        scratch_shapes=[
            *(pltpu.VMEM(a.shape, f32) for a in (field, theta, phi, phase, trans)),
            *(pltpu.VMEM(a.shape, jnp.int32) for a in (source, kind, count)),
            pltpu.VMEM((2, slots, members), jnp.int32),
            pltpu.SMEM((2, slots, members), jnp.int32),
            pltpu.SemaphoreType.DMA,
            pltpu.SemaphoreType.DMA((8,)),
            pltpu.VMEM(phase.shape, f32),
            pltpu.VMEM(phase.shape, f32),
            pltpu.VMEM((2, fine_t * coarse_p, columns), f32),
            pltpu.VMEM((members // 2, 2, columns, 4 * coarse_p), f32),
            pltpu.VMEM((2, fine_t * coarse_p, columns), f32),
            pltpu.VMEM((fine_t, 3 * coarse_t), bf16),
            pltpu.VMEM((2, 4 * coarse_p, 4 * fine_p), bf16),
            pltpu.VMEM((coarse_t, 3 * fine_t), bf16),
            pltpu.VMEM((4 * fine_p, 8 * coarse_p), bf16),
            pltpu.VMEM((kinds + 1, 2, *block), f32),
            pltpu.VMEM((chunks, members, *block), f32),
            *(pltpu.VMEM((3 * members, *block), f32) for _ in range(chunks)),
            pltpu.VMEM((chunks, members, *block), f32),
            pltpu.VMEM((chunks, members, *block), f32),
            pltpu.SemaphoreType.DMA((chunks,)),
            pltpu.SemaphoreType.DMA((chunks, 4)),
            pltpu.SemaphoreType.DMA((chunks, 2)),
            pltpu.SemaphoreType.DMA((chunks, 2)),
            pltpu.SemaphoreType.DMA((chunks,)),
            pltpu.SemaphoreType.DMA((chunks, members // 2)),
        ],
        compiler_params=pltpu.CompilerParams(
            collective_id=0, has_side_effects=True, vmem_limit_bytes=40 << 20
        ),
    )(*(pltpu.with_memory_space_constraint(a, pltpu.HBM) for a in (field, theta, phi, phase, trans, source, kind, count)))


def solution(mesh):
    groups, members = mesh.shape["grp"], mesh.shape["mem"]

    def run(field, theta, phi, phase, trans, source, kind, count):
        waves = field.shape[2] // phase.shape[0]
        return per_device(
            groups, members, waves, field, theta, phi, phase, trans, source, kind, count
        )

    return jax.shard_map(
        run,
        mesh=mesh,
        in_specs=(
            P(None, None, ("grp", "mem")),
            P(),
            P(),
            P(),
            P(None, None, "mem"),
            P("grp", None),
            P("grp", None),
            P("grp"),
        ),
        out_specs=P(None, None, ("grp", "mem")),
        check_vma=False,
    )
```
